32 devices in a mesh: groups: 2 (over y), wide: 4 (over z), narrow: 2 (over x), section: 2 (over core).
Axes of the slice: x: 2, y: 2, z: 4, core: 2. Of those that a mesh axis runs over, the one named last changes fastest.
Arguments:
- tokens: bfloat16 [1024, 4096], P(('groups', 'wide', 'section'), 'narrow'), parts along dimension 0, may hold values from -6 to 6
- route_logits: float32 [1024, 8], P(('groups', 'wide', 'section')), parts along dimension 0, may hold values from -8 to 8
- expert_ids: int32 [1024, 8], P(('groups', 'wide', 'section')), parts along dimension 0, may hold values from 0 to 63, all different within a row; in each aligned block of 64 rows (0 to 63, 64 to 127, ...) at most 12 rows name the same one
- gate_weight: bfloat16 [64, 4096, 768], P(('wide', 'section'), None, 'narrow'), may hold values from -0.09375 to 0.09375
- up_weight: bfloat16 [64, 4096, 768], P(('wide', 'section'), None, 'narrow'), may hold values from -0.09375 to 0.09375
- down_weight: bfloat16 [64, 768, 4096], P(('wide', 'section'), None, 'narrow'), may hold values from -0.21875 to 0.21875
Outputs:
- mixed: bfloat16 [1024, 4096], P(('groups', 'wide', 'section'), 'narrow'), parts along dimension 0
The draws below stay inside these ranges and needn't reach their ends.
There are 2 independent parts, one for each index of `groups`. The reference program is written for one: setup_inputs(seed, part) draws one part's arguments, and reference() takes and returns one part's arrays. A program takes and returns all parts, laid end to end along the dimension named above; an argument that names none is the same for every part. Nothing has to cross between parts.
Inputs may be any that keep to these rules, and one draw needn't show every extreme that they name: `expert_ids`: each row names 8 different experts; among the 64 rows of one aligned block no expert is named more than 12 times, a bound that some block reaches.
All inputs are finite; a program needn't handle non-finite values.
Results may differ from the reference program's by a relative error of at most 0.0085.
Values may be sent and summed in bfloat16 or wider, within the bound.
No kernel may reach another device: no remote copies, remote signals or barrier semaphores. Data moves between devices by JAX's collectives and lax.ppermute only.
A program may use at most 128 MiB of HBM per device.

```python
import math
import jax
import jax.numpy as jnp
import numpy as np
from jax import lax

D = 4096
FF = 768
EXPERTS = 64
TOPK = 8
TOK_DEV = 64
CAP = 12
TOKENS = 512


def shard_levels(own_key, dims, split, least, top_value):
    level = 1.0
    for axis_at, blocks in split:
        draws = jax.random.uniform(jax.random.fold_in(jax.random.fold_in(own_key, 6), axis_at), (blocks,), jnp.float32, least / len(split), top_value / len(split))
        level = level * jnp.repeat(jnp.exp(draws), dims[axis_at] // blocks).reshape((-1,) + (1,) * (len(dims) - 1 - axis_at))
    return level


def assign_block(stream_key, own, number, rows, count, top, limit, slope):
    ranking = jax.random.permutation(stream_key, count)
    packed, usual = portions_of(count, rows * top, limit, slope, True), portions_of(count, rows * top, limit, slope, False)
    places = jnp.arange(count)

    def named(tallies, offset_by):
        used = int((tallies > 0).sum())
        fixed = max(1, used // 4)
        moved = fixed + (places - fixed + offset_by * (used - fixed)) % max(1, count - fixed)
        return jnp.zeros((count,), jnp.int32).at[ranking[jnp.where(places < fixed, places, moved)]].set(jnp.asarray(tallies, jnp.int32))

    tallies = jnp.where(number % 4 == 0, named(packed, number // 4), named(usual, number - number // 4 - 1))
    mixed = jax.random.permutation(jax.random.fold_in(own, 3), count)
    giver, taker = mixed[0:count // 2 * 2:2], mixed[1:count // 2 * 2:2]
    slack = jnp.minimum(tallies[giver] - 1, limit - tallies[taker]) // 2
    slack = jnp.where((giver == ranking[0]) | (taker == ranking[0]) | (tallies[taker] == 0), 0, jnp.maximum(slack, 0))
    moved = jax.random.randint(jax.random.fold_in(own, 4), (count // 2,), 0, 1 << 20) % (slack + 1)
    tallies = tallies.at[giver].add(-moved).at[taker].add(moved)
    labels = jnp.searchsorted(jnp.cumsum(tallies), jnp.arange(rows * top), side="right").astype(jnp.int32)
    grid = labels.reshape(top, rows).T
    grid = grid[jax.random.permutation(jax.random.fold_in(own, 1), rows)]
    offset_by = jax.random.randint(jax.random.fold_in(own, 2), (rows, 1), 0, top)
    return jnp.take_along_axis(grid, (jnp.arange(top)[None, :] + offset_by) % top, axis=1)


def portions_of(count, total, reach, skew, full):
    loads = [(1 << 20) // math.isqrt(grade ** skew) + 1 for grade in range(1, count + 1)]
    largest = reach if full else min(reach, max(-(-total // count), total * loads[0] // sum(loads)))
    least = 1 if total - largest >= count - 1 else 0
    holding, rest = [largest] + [least] * (count - 1), total - largest - least * (count - 1)
    while rest > 0:
        free = [i for i in range(1, count) if holding[i] < largest] or [i for i in range(1, count) if holding[i] < reach]
        whole, left = sum([loads[i] for i in free]), rest
        for i in free:
            addition = min(reach - holding[i], max(1, left * loads[i] // whole), rest)
            holding[i] = holding[i] + addition
            rest = rest - addition
    return np.array(holding)


def normal_values(stream_key, extent, deviation, most, pieces=(), kind=jnp.bfloat16):
    factor_of = shard_levels(stream_key, extent, pieces, -0.22, 0.18) if pieces else 1.0
    array = jax.random.normal(stream_key, extent, jnp.float32) * deviation * factor_of
    return jnp.minimum(jnp.maximum(array, -most), most).astype(kind)


def setup_inputs(seed: int = 0, part: int = 0) -> dict:
    splits = jax.random.split(jax.random.key(seed), 7)
    part_splits = jax.random.split(jax.random.fold_in(splits[6], part), 7)
    tokens = normal_values(part_splits[0], (TOKENS, D), 1.0, 6.0, ((0, 8), (1, 2)))
    route_logits = normal_values(part_splits[1], (TOKENS, TOPK), 2.0, 8.0, ((0, 8),), jnp.float32)
    expert_ids_keys = jax.random.split(jax.random.fold_in(part_splits[2], 1), TOKENS // TOK_DEV)
    expert_ids_turns = jax.random.permutation(jax.random.fold_in(part_splits[2], 3), TOKENS // TOK_DEV)
    expert_ids = jax.vmap(lambda own, number: assign_block(jax.random.fold_in(part_splits[2], 2), own, number, TOK_DEV, EXPERTS, TOPK, CAP, 2))(expert_ids_keys, expert_ids_turns).reshape((TOKENS, TOPK))
    gate_weight = normal_values(splits[3], (EXPERTS, D, FF), D ** -0.5, 0.09375, ((0, 8), (2, 2)))
    up_weight = normal_values(splits[4], (EXPERTS, D, FF), D ** -0.5, 0.09375, ((0, 8), (2, 2)))
    down_weight = normal_values(splits[5], (EXPERTS, FF, D), FF ** -0.5, 0.21875, ((0, 8), (2, 2)))
    return dict(tokens=tokens, route_logits=route_logits, expert_ids=expert_ids, gate_weight=gate_weight, up_weight=up_weight, down_weight=down_weight)


def reference(tokens, route_logits, expert_ids, gate_weight, up_weight, down_weight):
    scores = jax.nn.sigmoid(route_logits.astype(jnp.float32))
    shares = (scores / jnp.sum(scores, axis=1, keepdims=True)).astype(jnp.bfloat16)
    blocks = TOKENS // TOK_DEV
    pair_ids = expert_ids.reshape(blocks, TOK_DEV * TOPK).astype(jnp.int32)
    one_hot = (pair_ids[:, :, None] == jnp.arange(EXPERTS, dtype=jnp.int32)[None, None, :]).astype(jnp.int32)
    slot_rank = jnp.sum(jnp.cumsum(one_hot, axis=1) * one_hot, axis=2) - 1
    slot_pos = (jnp.arange(blocks, dtype=jnp.int32)[:, None] * CAP + slot_rank).astype(jnp.int32)
    token_index = (jnp.arange(TOKENS * TOPK, dtype=jnp.int32) // TOPK).reshape(blocks, TOK_DEV * TOPK)
    list_rows = blocks * CAP
    row_table = jnp.full((EXPERTS, list_rows), TOKENS, jnp.int32)
    row_table = row_table.at[pair_ids.reshape(-1), slot_pos.reshape(-1)].set(token_index.reshape(-1))
    padded = jnp.concatenate([tokens, jnp.zeros((1, D), tokens.dtype)], axis=0)

    def expert(operands):
        indices, gate_mat, up_mat, down_mat = operands
        gathered = padded[indices]
        gate_val = jnp.dot(gathered, gate_mat, preferred_element_type=jnp.float32)
        up_val = jnp.dot(gathered, up_mat, preferred_element_type=jnp.float32)
        hidden = (jax.nn.silu(gate_val) * up_val).astype(jnp.bfloat16)
        return jnp.dot(hidden, down_mat, preferred_element_type=jnp.float32).astype(jnp.bfloat16)

    outputs = lax.map(expert, (row_table, gate_weight, up_weight, down_weight))
    picked = outputs[pair_ids.reshape(-1), slot_pos.reshape(-1)].reshape(TOKENS, TOPK, D)
    combined = jnp.einsum("tk,tkd->td", shares.astype(jnp.float32), picked.astype(jnp.float32))
    return combined.astype(jnp.bfloat16)
```

```python
import functools

import jax
import jax.numpy as jnp
from jax import lax
from jax.experimental import pallas as pl
from jax.experimental.pallas import tpu as pltpu
from jax.sharding import PartitionSpec as P

CAP = 12
LANES = 128


def shift(value, axis, step):
    count = lax.axis_size(axis)
    return lax.ppermute(value, axis, [(i, (i + step) % count) for i in range(count)])


def expert_shares(route_logits):
    scores = jax.nn.sigmoid(route_logits)
    return (scores / jnp.sum(scores, axis=1, keepdims=True)).astype(jnp.bfloat16)


def slot_plan(tokens, route_logits, expert_ids, gate_weight, up_weight, down_weight):
    tok_rows = tokens.shape[0]
    top_count = expert_ids.shape[1]
    feature_part = tokens.shape[1]
    owners = lax.axis_size("wide") * lax.axis_size("section")
    per_owner = gate_weight.shape[0]
    experts = owners * per_owner
    shares = expert_shares(route_logits)
    flat_ids = expert_ids.reshape(-1)
    one_hot = (flat_ids[:, None] == jnp.arange(experts, dtype=jnp.int32)[None, :]).astype(jnp.int32)
    slot_rank = jnp.sum(jnp.cumsum(one_hot, axis=0) * one_hot, axis=1) - 1
    columns = flat_ids * CAP + slot_rank
    placed = (columns[:, None] == jnp.arange(experts * CAP, dtype=jnp.int32)[None, :]).reshape(
        tok_rows, top_count, experts * CAP
    )
    dispatch = jnp.any(placed, axis=1).astype(jnp.bfloat16)
    outgoing = jnp.einsum("rs,rd->sd", dispatch, tokens, preferred_element_type=jnp.float32).astype(
        jnp.bfloat16
    )
    combine = jnp.sum(
        jnp.where(placed, shares.astype(jnp.float32)[:, :, None], 0.0), axis=1
    ).astype(jnp.bfloat16)
    arrived = lax.all_to_all(
        outgoing.reshape(owners, per_owner, CAP, feature_part),
        ("wide", "section"),
        split_axis=0,
        concat_axis=0,
        tiled=True,
    )
    portion = lax.all_gather(arrived, "narrow", axis=3, tiled=True)
    gate_add = jnp.einsum(
        "gjcd,jdf->gjcf", portion, gate_weight, preferred_element_type=jnp.float32
    )
    up_add = jnp.einsum("gjcd,jdf->gjcf", portion, up_weight, preferred_element_type=jnp.float32)
    hidden = (jax.nn.silu(gate_add) * up_add).astype(jnp.bfloat16)
    summed = jnp.einsum(
        "gjcf,jfd->gjcd",
        lax.all_gather(hidden, "narrow", axis=3, tiled=True),
        down_weight,
        preferred_element_type=jnp.float32,
    ).astype(jnp.bfloat16)
    returned = lax.all_to_all(summed, ("wide", "section"), split_axis=0, concat_axis=0, tiled=True)
    returned = returned.reshape(experts * CAP, feature_part)
    return jnp.dot(combine, returned, preferred_element_type=jnp.float32).astype(jnp.bfloat16)


def routing_body(base_ref, *refs, per_owner, tok_rows, top_count):
    meta_refs, (place_ref, combine_ref) = refs[:-2], refs[-2:]
    meta = jnp.concatenate(
        [r[...].reshape(-1, LANES).astype(jnp.float32) for r in meta_refs], axis=0
    )
    rows = meta.shape[0]
    list_rows = rows // tok_rows * CAP
    lane = lax.broadcasted_iota(jnp.int32, (rows, LANES), 1)
    ids = pltpu.roll(meta, LANES - top_count, 1)
    base = base_ref[0]
    member = jnp.zeros((rows, LANES), jnp.float32)
    weight = jnp.zeros((rows, LANES), jnp.float32)
    for e in range(per_owner):
        hit = (ids == (base + e).astype(jnp.float32)) & (lane < top_count)
        found = jnp.max(jnp.where(hit, 1.0, 0.0), axis=1, keepdims=True)
        share = jnp.sum(jnp.where(hit, meta, 0.0), axis=1, keepdims=True)
        member = jnp.where(lane == e, found, member)
        weight = jnp.where(lane == e, share, weight)
    r = lax.broadcasted_iota(jnp.int32, (rows, rows), 0)
    c = lax.broadcasted_iota(jnp.int32, (rows, rows), 1)
    earlier = jnp.where((c < r) & (c // tok_rows == r // tok_rows), 1.0, 0.0)
    rank = jnp.dot(
        earlier.astype(jnp.bfloat16), member.astype(jnp.bfloat16), preferred_element_type=jnp.float32
    )
    block = lax.broadcasted_iota(jnp.int32, (rows, LANES), 0) // tok_rows
    place = jnp.where(member > 0.0, rank.astype(jnp.int32) + block * CAP, -1)
    flipped = jnp.transpose(place.astype(jnp.float32)).astype(jnp.int32)
    slot_lane = lax.broadcasted_iota(jnp.int32, (rows, per_owner * list_rows), 1)
    combine = jnp.zeros((rows, per_owner * list_rows), jnp.float32)
    for e in range(per_owner):
        place_ref[e] = flipped[e : e + 1]
        column = jnp.where(place[:, e : e + 1] >= 0, place[:, e : e + 1] + e * list_rows, -1)
        combine = jnp.where(slot_lane == column, weight[:, e : e + 1], combine)
    combine_ref[...] = combine.astype(jnp.bfloat16)


def routing(base, stacks, per_owner, tok_rows, top_count):
    wide_count = stacks[0].shape[0]
    rows = len(stacks) * wide_count * tok_rows
    list_rows = rows // tok_rows * CAP
    meta_at = stacks[0].shape[2] // LANES - 1
    spec = pl.BlockSpec((wide_count, tok_rows, LANES), lambda i, b: (0, 0, meta_at))
    return pl.pallas_call(
        functools.partial(
            routing_body, per_owner=per_owner, tok_rows=tok_rows, top_count=top_count
        ),
        out_shape=(
            jax.ShapeDtypeStruct((per_owner, 1, rows), jnp.int32),
            jax.ShapeDtypeStruct((rows, per_owner * list_rows), jnp.bfloat16),
        ),
        grid_spec=pltpu.PrefetchScalarGridSpec(
            num_scalar_prefetch=1,
            grid=(1,),
            in_specs=[spec] * len(stacks),
            out_specs=(
                pl.BlockSpec((per_owner, 1, rows), lambda i, b: (0, 0, 0)),
                pl.BlockSpec((rows, per_owner * list_rows), lambda i, b: (0, 0)),
            ),
        ),
        name="routing",
    )(base, *stacks)


def gate_up_body(part_ref, *refs, stack_count, has_sum, last):
    stacks, refs = refs[:stack_count], refs[stack_count:]
    place_ref, gate_ref, up_ref = refs[:3]
    refs = refs[3:]
    list_rows = refs[0].shape[1]
    place = place_ref[0]
    rows = place.shape[1]
    pick = jnp.where(
        lax.broadcasted_iota(jnp.int32, (list_rows, rows), 0) == place, 1.0, 0.0
    ).astype(jnp.bfloat16)
    each = rows // stack_count
    picked = None
    for k, stack in enumerate(stacks):
        block = stack[...].reshape(each, stack.shape[2])
        term = jnp.dot(pick[:, k * each : (k + 1) * each], block, preferred_element_type=jnp.float32)
        picked = term if picked is None else picked + term
    picked = picked.astype(jnp.bfloat16)
    gate = jnp.dot(picked, gate_ref[0], preferred_element_type=jnp.float32)
    up = jnp.dot(picked, up_ref[0], preferred_element_type=jnp.float32)
    if has_sum:
        gate = gate + refs[0][0]
        up = up + refs[1][0]
        refs = refs[2:]
    if last:
        refs[0][0] = (jax.nn.silu(gate) * up).astype(jnp.bfloat16)
    else:
        refs[0][0] = gate
        refs[1][0] = up


def gate_up(part, stacks, place, gate_weight, up_weight, sums, width, first, count, last):
    hidden_part = gate_weight.shape[2]
    wide_count, tok_rows = stacks[0].shape[:2]
    rows = place.shape[2]
    list_rows = rows // tok_rows * CAP
    stack_spec = pl.BlockSpec((wide_count, tok_rows, width), lambda e, p: (0, 0, 0))
    place_spec = pl.BlockSpec((1, 1, rows), lambda e, p: (e + first, 0, 0))
    weight_spec = pl.BlockSpec((1, width, hidden_part), lambda e, p: (e + first, p[0], 0))
    in_sum_spec = pl.BlockSpec((1, list_rows, hidden_part), lambda e, p: (e + first, 0, 0))
    out_spec = pl.BlockSpec((1, list_rows, hidden_part), lambda e, p: (e, 0, 0))
    shape = (count, list_rows, hidden_part)
    if last:
        out_shape, out_specs = jax.ShapeDtypeStruct(shape, jnp.bfloat16), out_spec
    else:
        out_shape = (jax.ShapeDtypeStruct(shape, jnp.float32),) * 2
        out_specs = (out_spec,) * 2
    flops = 2 * count * list_rows * width * (2 * hidden_part + rows)
    return pl.pallas_call(
        functools.partial(
            gate_up_body, stack_count=len(stacks), has_sum=bool(sums), last=last
        ),
        out_shape=out_shape,
        grid_spec=pltpu.PrefetchScalarGridSpec(
            num_scalar_prefetch=1,
            grid=(count,),
            in_specs=[stack_spec] * len(stacks)
            + [place_spec, weight_spec, weight_spec]
            + [in_sum_spec] * len(sums),
            out_specs=out_specs,
        ),
        cost_estimate=pl.CostEstimate(
            flops=flops, transcendentals=0, bytes_accessed=4 * count * width * hidden_part
        ),
        name="gate_up",
    )(part, *stacks, place, gate_weight, up_weight, *sums)


def down_body(parts_ref, *refs, narrow_count, groups, wide_count):
    hidden_refs = refs[: narrow_count * groups]
    weight_refs = refs[narrow_count * groups : narrow_count * (groups + 1)]
    combine_ref, own_ref, send_ref, out_scratch = refs[narrow_count * (groups + 1) :]
    in_group, list_rows = hidden_refs[0].shape[:2]
    for g in range(groups):
        for j in range(in_group):
            e = g * in_group + j
            total = None
            for k in range(narrow_count):
                term = jnp.dot(
                    hidden_refs[k * groups + g][j], weight_refs[k][e], preferred_element_type=jnp.float32
                )
                total = term if total is None else total + term
            out_scratch[e * list_rows : (e + 1) * list_rows, :] = total.astype(jnp.bfloat16)
    part = jnp.dot(combine_ref[...], out_scratch[...], preferred_element_type=jnp.float32)
    own_rows = part.shape[0] // (1 + send_ref.shape[0])
    own_ref[...] = part[:own_rows]
    for k in range(send_ref.shape[0]):
        send_ref[k] = part[(k + 1) * own_rows : (k + 2) * own_rows].astype(jnp.bfloat16)


def down(parts, hidden, down_weight, combine, tile, first_tile, tiles, section_count, wide_count):
    narrow_count, groups = len(hidden), len(hidden[0])
    in_group, list_rows, hidden_part = hidden[0][0].shape
    per_owner = down_weight.shape[0]
    rows = combine.shape[0]
    own_rows = rows // section_count
    whole = lambda shape: pl.BlockSpec(shape, lambda f, p: (0,) * len(shape))
    weight_specs = [
        pl.BlockSpec(
            (per_owner, hidden_part, tile), lambda f, p, k=k: (0, p[k], f + first_tile)
        )
        for k in range(narrow_count)
    ]
    width = tile * tiles
    return pl.pallas_call(
        functools.partial(
            down_body, narrow_count=narrow_count, groups=groups, wide_count=wide_count
        ),
        out_shape=(
            jax.ShapeDtypeStruct((own_rows, width), jnp.float32),
            jax.ShapeDtypeStruct((section_count - 1, own_rows, width), jnp.bfloat16),
        ),
        grid_spec=pltpu.PrefetchScalarGridSpec(
            num_scalar_prefetch=1,
            grid=(tiles,),
            in_specs=[whole(hidden[0][0].shape)] * (narrow_count * groups)
            + weight_specs
            + [whole(combine.shape)],
            out_specs=(
                pl.BlockSpec((own_rows, tile), lambda f, p: (0, f)),
                pl.BlockSpec((section_count - 1, own_rows, tile), lambda f, p: (0, 0, f)),
            ),
            scratch_shapes=[pltpu.VMEM((per_owner * list_rows, tile), jnp.bfloat16)],
        ),
        cost_estimate=pl.CostEstimate(
            flops=2 * per_owner * list_rows * width * (hidden_part * narrow_count + rows),
            transcendentals=0,
            bytes_accessed=2 * per_owner * narrow_count * hidden_part * width,
        ),
        name="down",
    )(parts, *[h for side in hidden for h in side], *[down_weight] * narrow_count, combine)


def gather_plan(tokens, route_logits, expert_ids, gate_weight, up_weight, down_weight):
    tok_rows, feature_part = tokens.shape
    top_count = expert_ids.shape[1]
    wide_count = lax.axis_size("wide")
    section_count = lax.axis_size("section")
    narrow_count = lax.axis_size("narrow")
    per_owner = gate_weight.shape[0]
    narrow_at = lax.axis_index("narrow")
    base = (lax.axis_index("wide") * section_count + lax.axis_index("section")) * per_owner
    pieces = 2
    width = feature_part // pieces
    meta = jnp.concatenate(
        [
            expert_shares(route_logits),
            expert_ids.astype(jnp.bfloat16),
            jnp.zeros((tok_rows, LANES - 2 * top_count), jnp.bfloat16),
        ],
        axis=1,
    )
    chunks = {}
    for q in range(pieces):
        block = tokens[:, q * width : (q + 1) * width]
        if q == 0:
            block = jnp.concatenate([block, meta], axis=1)
        near = [block] + [shift(block, "wide", d) for d in range(1, wide_count)]
        for j in range(narrow_count):
            side = near
            if j:
                side = [shift(b, "narrow", j) for b in near]
            stack = jnp.stack(side)
            chunks[j, q] = [stack] + [shift(stack, "section", k) for k in range(1, section_count)]
    place, combine = routing(
        base.astype(jnp.int32).reshape(1), chunks[0, 0], per_owner, tok_rows, top_count
    )
    order = [(j, q) for j in range(narrow_count) for q in range(pieces)]
    sums = ()
    for j, q in order[:-1]:
        part = ((narrow_at - j) % narrow_count * pieces + q).astype(jnp.int32).reshape(1)
        sums = gate_up(
            part, chunks[j, q], place, gate_weight, up_weight, sums, width, 0, per_owner, False
        )
    groups = 2 if per_owner % 2 == 0 else 1
    in_group = per_owner // groups
    j, q = order[-1]
    part = ((narrow_at - j) % narrow_count * pieces + q).astype(jnp.int32).reshape(1)
    mine = [
        gate_up(
            part, chunks[j, q], place, gate_weight, up_weight, sums, width, g * in_group, in_group, True
        )
        for g in range(groups)
    ]
    hidden = [mine] + [[shift(h, "narrow", k) for h in mine] for k in range(1, narrow_count)]
    parts = jnp.stack([(narrow_at - k) % narrow_count for k in range(narrow_count)]).astype(jnp.int32)
    tile = 256
    spans = 2
    tiles = feature_part // tile // spans
    outs = []
    for s in range(spans):
        own, send = down(
            parts, hidden, down_weight, combine, tile, s * tiles, tiles, section_count, wide_count
        )
        total = own
        for k in range(1, section_count):
            total = total + shift(send[k - 1], "section", section_count - k).astype(jnp.float32)
        total = total.reshape(wide_count, tok_rows, -1)
        mixed = total[0]
        for d in range(1, wide_count):
            mixed = mixed + shift(total[d].astype(jnp.bfloat16), "wide", wide_count - d).astype(
                jnp.float32
            )
        outs.append(mixed.astype(jnp.bfloat16))
    return jnp.concatenate(outs, axis=1)


def shards(tokens, route_logits, expert_ids, gate_weight, up_weight, down_weight):
    owners = lax.axis_size("wide") * lax.axis_size("section")
    per_owner = gate_weight.shape[0]
    whole_rows = per_owner * CAP >= tokens.shape[0]
    exact_ids = owners * per_owner <= 256
    plan = gather_plan if whole_rows and exact_ids else slot_plan
    return plan(tokens, route_logits, expert_ids, gate_weight, up_weight, down_weight)


def solution(mesh):
    in_specs = (
        P(("groups", "wide", "section"), "narrow"),
        P(("groups", "wide", "section"), None),
        P(("groups", "wide", "section"), None),
        P(("wide", "section"), None, "narrow"),
        P(("wide", "section"), None, "narrow"),
        P(("wide", "section"), None, "narrow"),
    )
    out_specs = P(("groups", "wide", "section"), "narrow")
    return jax.shard_map(shards, mesh=mesh, in_specs=in_specs, out_specs=out_specs, check_vma=False)
```

```python
import functools
import math

import jax
import jax.numpy as jnp
from jax import lax
from jax.experimental import pallas as pl
from jax.experimental.pallas import tpu as pltpu
from jax.sharding import PartitionSpec as P


CAP = 12
LANES = 128
KERNEL_VMEM = 4 << 20
RESIDENT = 48 << 20
TILE = 256


def shift(value, axis, step):
    count = lax.axis_size(axis)
    return lax.ppermute(value, axis, [(i, (i + step) % count) for i in range(count)])


def pass_on(value, step):
    count = lax.axis_size("wide")
    ring = [0, *range(1, count, 2), *reversed(range(2, count, 2))]
    return lax.ppermute(value, "wide", [(ring[i], ring[(i + step) % count]) for i in range(count)])


def expert_shares(route_logits):
    scores = jax.nn.sigmoid(route_logits)
    return (scores / jnp.sum(scores, axis=1, keepdims=True)).astype(jnp.bfloat16)


def slot_plan(tokens, route_logits, expert_ids, gate_weight, up_weight, down_weight):
    tok_rows = tokens.shape[0]
    top_count = expert_ids.shape[1]
    feature_part = tokens.shape[1]
    owners = lax.axis_size("wide") * lax.axis_size("section")
    per_owner = gate_weight.shape[0]
    experts = owners * per_owner
    shares = expert_shares(route_logits)
    flat_ids = expert_ids.reshape(-1)
    one_hot = (flat_ids[:, None] == jnp.arange(experts, dtype=jnp.int32)[None, :]).astype(jnp.int32)
    slot_rank = jnp.sum(jnp.cumsum(one_hot, axis=0) * one_hot, axis=1) - 1
    columns = flat_ids * CAP + slot_rank
    placed = (columns[:, None] == jnp.arange(experts * CAP, dtype=jnp.int32)[None, :]).reshape(
        tok_rows, top_count, experts * CAP
    )
    dispatch = jnp.any(placed, axis=1).astype(jnp.bfloat16)
    outgoing = jnp.einsum("rs,rd->sd", dispatch, tokens, preferred_element_type=jnp.float32).astype(
        jnp.bfloat16
    )
    combine = jnp.sum(
        jnp.where(placed, shares.astype(jnp.float32)[:, :, None], 0.0), axis=1
    ).astype(jnp.bfloat16)
    arrived = lax.all_to_all(
        outgoing.reshape(owners, per_owner, CAP, feature_part),
        ("wide", "section"),
        split_axis=0,
        concat_axis=0,
        tiled=True,
    )
    portion = lax.all_gather(arrived, "narrow", axis=3, tiled=True)
    gate_add = jnp.einsum(
        "gjcd,jdf->gjcf", portion, gate_weight, preferred_element_type=jnp.float32
    )
    up_add = jnp.einsum("gjcd,jdf->gjcf", portion, up_weight, preferred_element_type=jnp.float32)
    hidden = (jax.nn.silu(gate_add) * up_add).astype(jnp.bfloat16)
    summed = jnp.einsum(
        "gjcf,jfd->gjcd",
        lax.all_gather(hidden, "narrow", axis=3, tiled=True),
        down_weight,
        preferred_element_type=jnp.float32,
    ).astype(jnp.bfloat16)
    returned = lax.all_to_all(summed, ("wide", "section"), split_axis=0, concat_axis=0, tiled=True)
    returned = returned.reshape(experts * CAP, feature_part)
    return jnp.dot(combine, returned, preferred_element_type=jnp.float32).astype(jnp.bfloat16)


def call(body, out_shape, inputs, spaces, scratch=(), flops=10**6, moved=10**6, fetch=None):
    vmem = pl.BlockSpec(memory_space=pltpu.VMEM)
    hbm = pl.BlockSpec(memory_space=pltpu.HBM)
    spec = {"s": pl.BlockSpec(memory_space=pltpu.SMEM), "v": vmem, "h": hbm}
    in_specs = [spec[c] for c in spaces]
    outs = out_shape if isinstance(out_shape, tuple) else (out_shape,)
    run, ins = body, len(inputs)
    if fetch:
        sources, shape, copies, count = fetch
        in_specs += [hbm] * len(sources)
        outs += (pltpu.VMEM(shape, jnp.bfloat16),)
        scratch = (*scratch, pltpu.SemaphoreType.DMA((count,)))
        inputs = (*inputs, *sources)
        from_hbm = len(sources)

        def run(*refs):
            mine, refs = refs[:ins], refs[ins:]
            weights, refs = refs[:from_hbm], refs[from_hbm:]
            results, refs = refs[: len(outs) - 1], refs[len(outs) - 1 :]
            target, rest, sems = refs[0], refs[1:-1], refs[-1]
            for copy in copies(mine[0], weights, target, sems):
                copy.start()
            if body is not None:
                body(*mine, *results, *rest)
            for copy in copies(mine[0], weights, target, sems):
                copy.wait()

        moved += 2 * math.prod(shape)
    result = pl.pallas_call(
        run,
        out_shape=outs,
        in_specs=in_specs,
        out_specs=(vmem,) * len(outs),
        scratch_shapes=scratch,
        compiler_params=pltpu.CompilerParams(vmem_limit_bytes=KERNEL_VMEM),
        cost_estimate=pl.CostEstimate(flops=flops, transcendentals=0, bytes_accessed=moved),
    )(*inputs)
    return result if len(outs) > 1 else result[0]


def gate_up_fetch(gate_weight, up_weight, width, side, piece, narrow_count, first, count):
    _, features, hidden_part = gate_weight.shape

    def copies(narrow_ref, sources, target, sems):
        part = (narrow_ref[0] + narrow_count - side) % narrow_count
        rows = pl.ds(pl.multiple_of(part * (features // narrow_count) + piece * width, width), width)
        return [
            pltpu.make_async_copy(
                source.at[first + e, rows, :],
                target.at[e, :, pl.ds(h * hidden_part, hidden_part)],
                sems.at[e * 2 + h],
            )
            for e in range(count)
            for h, source in enumerate(sources)
        ]

    return (gate_weight, up_weight), (count, width, 2 * hidden_part), copies, 2 * count


def array(shape, kind=jnp.bfloat16):
    return jax.ShapeDtypeStruct(shape, kind)


def pack_body(token_hbm, logit_hbm, id_hbm, out_ref, logit_ref, id_ref, sems, *, width):
    rest = token_hbm.shape[1] - width
    copies = [
        pltpu.make_async_copy(logit_hbm, logit_ref, sems.at[0]),
        pltpu.make_async_copy(id_hbm, id_ref, sems.at[1]),
        pltpu.make_async_copy(
            token_hbm.at[:, pl.ds(0, width)], out_ref.at[:, pl.ds(0, width)], sems.at[2]
        ),
        pltpu.make_async_copy(
            token_hbm.at[:, pl.ds(width, rest)],
            out_ref.at[:, pl.ds(width + LANES, rest)],
            sems.at[3],
        ),
    ]
    for copy in copies:
        copy.start()
    for copy in copies[:2]:
        copy.wait()
    scores = jax.nn.sigmoid(logit_ref[...])
    shares = scores / jnp.sum(scores, axis=0, keepdims=True)
    top_count, tok_rows = shares.shape
    out_ref[:, width : width + LANES] = jnp.zeros((tok_rows, LANES), jnp.bfloat16)
    meta = jnp.concatenate([shares, id_ref[...].astype(jnp.float32)], axis=0)
    out_ref[: 2 * top_count, width : width + tok_rows] = meta.astype(jnp.bfloat16)
    for copy in copies[2:]:
        copy.wait()


def pack(tokens, route_logits, expert_ids, width):
    tok_rows, feature_part = tokens.shape
    top_count = expert_ids.shape[1]
    sources = [
        pltpu.with_memory_space_constraint(x, pltpu.HBM)
        for x in (tokens, route_logits.T, expert_ids.T)
    ]
    return call(
        functools.partial(pack_body, width=width),
        array((tok_rows, feature_part + LANES)),
        sources,
        "hhh",
        [
            pltpu.VMEM((top_count, tok_rows), jnp.float32),
            pltpu.VMEM((top_count, tok_rows), jnp.int32),
            pltpu.SemaphoreType.DMA((4,)),
        ],
    )


def split_body(block_ref, *outs):
    start = 0
    for out in outs:
        out[...] = block_ref[:, start : start + out.shape[1]]
        start += out.shape[1]


def split_block(block, width, pieces):
    shapes = [array((block.shape[0], width + (LANES if q == 0 else 0))) for q in range(pieces)]
    return call(split_body, tuple(shapes), (block,), "v")


def stack_body(*refs, start):
    *blocks, last, out = refs
    width = out.shape[2]
    for d, block in enumerate(blocks):
        out[d] = block[:, start : start + width]
    out[len(blocks)] = last[...]


def stack_blocks(blocks, last, start):
    return call(
        functools.partial(stack_body, start=start),
        array((len(blocks) + 1,) + last.shape),
        (*blocks, last),
        "v" * (len(blocks) + 1),
    )


def distance_groups():
    count = lax.axis_size("wide")
    if count % 2:
        return [slice(0, count)]
    return [slice(count // 2, count), slice(0, count // 2)]


def routing_body(narrow_ref, base_ref, *refs, per_owner, tok_rows, top_count, groups):
    outs = 2 + len(groups)
    meta_refs, (place_ref, share_ref, *pick_refs) = refs[:-outs], refs[-outs:]
    r = lax.broadcasted_iota(jnp.int32, (tok_rows, tok_rows), 0)
    c = lax.broadcasted_iota(jnp.int32, (tok_rows, tok_rows), 1)
    earlier = jnp.where(r < c, 1.0, 0.0).astype(jnp.bfloat16)
    base = base_ref[0]
    order = [(m, d) for g in groups for m in meta_refs for d in range(g.start, g.stop)]
    for block, (meta_ref, d) in enumerate(order):
        at = meta_ref.shape[2] - LANES
        meta = meta_ref[d, : 2 * top_count, at : at + tok_rows].astype(jnp.float32)
        shares, ids = meta[:top_count], meta[top_count:]
        found, weight = [], []
        for e in range(per_owner):
            hit = ids == (base + e).astype(jnp.float32)
            found.append(jnp.max(jnp.where(hit, 1.0, 0.0), axis=0, keepdims=True))
            weight.append(jnp.sum(jnp.where(hit, shares, 0.0), axis=0, keepdims=True))
        member = jnp.concatenate(found, axis=0)
        rank = jnp.dot(member.astype(jnp.bfloat16), earlier, preferred_element_type=jnp.float32)
        place = jnp.where(member > 0.0, rank + float(block * CAP), -1.0).astype(jnp.int32)
        lanes = slice(block * tok_rows, (block + 1) * tok_rows)
        for e in range(per_owner):
            place_ref[e, :, lanes] = place[e : e + 1]
            share_ref[e, :, lanes] = weight[e]
    each = place_ref.shape[2] // len(groups)
    list_each = pick_refs[0].shape[1]
    row = lax.broadcasted_iota(jnp.int32, (list_each, each), 0)
    for g, pick_ref in enumerate(pick_refs):
        for e in range(per_owner):
            place = place_ref[e, :, g * each : (g + 1) * each]
            pick_ref[e] = jnp.where(row + g * list_each == place, 1.0, 0.0).astype(jnp.bfloat16)


def routing(narrow_at, base, stacks, per_owner, tok_rows, top_count):
    rows = len(stacks) * stacks[0].shape[0] * tok_rows
    count = len(distance_groups())
    return call(
        functools.partial(
            routing_body,
            per_owner=per_owner,
            tok_rows=tok_rows,
            top_count=top_count,
            groups=distance_groups(),
        ),
        (array((per_owner, 1, rows), jnp.int32), array((per_owner, 1, rows), jnp.float32))
        + (array((per_owner, rows // tok_rows * CAP // count, rows // count)),) * count,
        (narrow_at, base, *stacks),
        "ss" + "v" * len(stacks),
    )


def combine_body(place_ref, share_ref, *combine_refs):
    per_owner, _, rows = place_ref.shape
    each = rows // len(combine_refs)
    list_each = combine_refs[0].shape[1] // per_owner
    row = lax.broadcasted_iota(jnp.int32, (list_each, each), 0)
    for g, combine_ref in enumerate(combine_refs):
        lanes = slice(g * each, (g + 1) * each)
        table = jnp.concatenate(
            [
                jnp.where(row + g * list_each == place_ref[e, :, lanes], share_ref[e, :, lanes], 0.0)
                for e in range(per_owner)
            ],
            axis=0,
        )
        combine_ref[...] = jnp.transpose(table).astype(jnp.bfloat16)


def combine_tables(place, share, list_rows):
    per_owner, _, rows = place.shape
    count = len(distance_groups())
    return call(
        combine_body,
        (array((rows // count, per_owner * list_rows // count)),) * count,
        (place, share),
        "vv",
    )


def gate_up_body(narrow_ref, *refs, stack_count, kept, groups, has_sum, joins, width, first, last):
    stacks, refs = refs[:stack_count], refs[stack_count:]
    pick_refs, refs = refs[: len(groups)], refs[len(groups) :]
    weight_refs, refs = refs[:kept], refs[kept:]
    held = [r.at[e] for r in weight_refs for e in range(r.shape[0])]
    sum_ref, refs = (refs[0], refs[1:]) if has_sum else (None, refs)
    joined, refs = refs[:joins], refs[joins:]
    out_refs, picked = refs[:-1], refs[-1]
    for have, out_ref in zip(joined, out_refs[1:]):
        out_ref[:first] = have[...]
    count, list_rows = picked.shape[:2]
    list_each = list_rows // len(groups)
    for g, where in enumerate(groups):
        pick = pick_refs[g][first : first + count].reshape(count * list_each, -1)
        token = jnp.concatenate([s[where, :, :width].reshape(-1, width) for s in stacks], axis=0)
        found = jnp.dot(pick, token, preferred_element_type=jnp.float32).astype(jnp.bfloat16)
        for e in range(count):
            picked[e, g * list_each : (g + 1) * list_each, :] = found[
                e * list_each : (e + 1) * list_each
            ]
    hidden_part = weight_refs[0].shape[2] // 2
    for e in range(count):
        both = jnp.dot(picked[e], held[e][...], preferred_element_type=jnp.float32)
        if has_sum:
            both = both + sum_ref[first + e]
        if not last:
            out_refs[0][e] = both
            continue
        hidden = (jax.nn.silu(both[:, :hidden_part]) * both[:, hidden_part:]).astype(jnp.bfloat16)
        for g, out_ref in enumerate(out_refs):
            at = first + e if g and joins else e
            out_ref[at] = hidden[g * list_each : (g + 1) * list_each]


def gate_up(narrow_at, stacks, picks, weights, sums, width, first=0, last=False, joined=(), fetch=None):
    count, list_rows = sum(w.shape[0] for w in weights), sum(p.shape[1] for p in picks)
    both = weights[0].shape[2]
    groups = distance_groups()
    rows = sum(p.shape[2] for p in picks)
    if last:
        shape = (list_rows // len(groups), both // 2)
        late_count = count + first if joined else count
        out_shape = (array((count,) + shape),) + (array((late_count,) + shape),) * (len(groups) - 1)
    else:
        out_shape = pltpu.VMEM((count, list_rows, both), jnp.float32)
    extra = (() if sums is None else (sums,)) + tuple(joined)
    return call(
        functools.partial(
            gate_up_body,
            stack_count=len(stacks),
            kept=len(weights),
            groups=groups,
            has_sum=sums is not None,
            joins=len(joined),
            width=width,
            first=first,
            last=last,
        ),
        out_shape,
        (narrow_at, *stacks, *picks, *weights, *extra),
        "s" + "v" * (len(stacks) + len(picks) + len(weights) + len(extra)),
        [pltpu.VMEM((count, list_rows, width), jnp.bfloat16)],
        2 * count * list_rows * width * (both + rows),
        2 * count * width * both,
        fetch,
    )


def down_body(narrow_ref, *refs, narrow_count, parts, start):
    hidden_refs, refs = refs[: narrow_count * parts], refs[narrow_count * parts :]
    combine_ref, down_ref, own_ref, send_ref, hidden_all, outs = refs
    list_rows, hidden_part = hidden_refs[0].shape[1:]
    count = 0
    for i in range(parts):
        experts = hidden_refs[i].shape[0]
        for p in range(narrow_count):
            part = hidden_refs[i][...]
            for k in range(1, narrow_count):
                mine = (narrow_ref[0] + narrow_count - k) % narrow_count == p
                part = jnp.where(mine, hidden_refs[k * parts + i][...], part)
            hidden_all[count : count + experts, :, p * hidden_part : (p + 1) * hidden_part] = part
        count += experts
    for f in range(0, own_ref.shape[1], TILE):
        at = slice(f, f + TILE)
        for e in range(count):
            outs[e * list_rows : (e + 1) * list_rows, :] = jnp.dot(
                hidden_all[e],
                down_ref[e, :, start + f : start + f + TILE],
                preferred_element_type=jnp.float32,
            ).astype(jnp.bfloat16)
        weigh(combine_ref, outs, own_ref, send_ref, at)


def weigh(combine_ref, outs, own_ref, send_ref, at):
    part = jnp.dot(combine_ref[...], outs[...], preferred_element_type=jnp.float32)
    own_rows = own_ref.shape[0]
    own_ref[:, at] = part[:own_rows]
    for k in range(send_ref.shape[0]):
        send_ref[k, :, at] = part[(k + 1) * own_rows : (k + 2) * own_rows].astype(jnp.bfloat16)


def own_half_body(narrow_ref, *refs):
    *hidden_refs, down_ref, out_ref = refs
    list_rows, hidden_part = hidden_refs[0].shape[1:]
    units = pl.ds(pl.multiple_of(narrow_ref[0] * hidden_part, hidden_part), hidden_part)
    experts = [r.at[j] for r in hidden_refs for j in range(r.shape[0])]
    for f in range(0, out_ref.shape[1], TILE):
        at = slice(f, f + TILE)
        for e, hidden in enumerate(experts):
            out_ref[e * list_rows : (e + 1) * list_rows, at] = jnp.dot(
                hidden[...], down_ref[e, units, at], preferred_element_type=jnp.float32
            )


def other_half_body(narrow_ref, *refs, narrow_count, parts, start):
    hidden_refs, refs = refs[: (narrow_count - 1) * parts], refs[(narrow_count - 1) * parts :]
    combine_ref, down_ref, half_ref, own_ref, send_ref, outs = refs
    list_rows, hidden_part = hidden_refs[0].shape[1:]
    sides = []
    for k in range(1, narrow_count):
        place = (narrow_ref[0] + narrow_count - k) % narrow_count
        units = pl.ds(pl.multiple_of(place * hidden_part, hidden_part), hidden_part)
        side = hidden_refs[(k - 1) * parts : k * parts]
        sides.append((units, [r.at[j] for r in side for j in range(r.shape[0])]))
    for f in range(0, own_ref.shape[1], TILE):
        columns = slice(start + f, start + f + TILE)
        for e in range(down_ref.shape[0]):
            rows = slice(e * list_rows, (e + 1) * list_rows)
            total = half_ref[rows, columns]
            for units, experts in sides:
                total = total + jnp.dot(
                    experts[e][...], down_ref[e, units, columns], preferred_element_type=jnp.float32
                )
            outs[rows, :] = total.astype(jnp.bfloat16)
        weigh(combine_ref, outs, own_ref, send_ref, slice(f, f + TILE))


def own_half(narrow_at, own, down_weight):
    count, _, feature_part = down_weight.shape
    list_rows, hidden_part = own[0].shape[1:]
    return call(
        own_half_body,
        pltpu.VMEM((count * list_rows, feature_part), jnp.float32),
        (narrow_at, *own, down_weight),
        "s" + "v" * (len(own) + 1),
        (),
        2 * count * list_rows * feature_part * hidden_part,
        2 * count * hidden_part * feature_part,
    )


def down(narrow_at, hidden, down_weight, combine, start, width, section_count, half=None):
    narrow_count, parts = len(hidden), len(hidden[0])
    list_rows = hidden[0][0].shape[1]
    count, hidden_all, _ = down_weight.shape
    rows = combine.shape[0]
    own_rows = rows // section_count
    body = down_body if half is None else other_half_body
    scratch = [pltpu.VMEM((count * list_rows, TILE), jnp.bfloat16)]
    inputs = [h for side in hidden for h in side]
    if half is None:
        scratch.insert(0, pltpu.VMEM((count, list_rows, hidden_all), jnp.bfloat16))
        inputs += [combine, down_weight]
    else:
        inputs = inputs[parts:] + [combine, down_weight, half]
    return call(
        functools.partial(body, narrow_count=narrow_count, parts=parts, start=start),
        (array((own_rows, width), jnp.float32), array((section_count - 1, own_rows, width))),
        (narrow_at, *inputs),
        "s" + "v" * len(inputs),
        scratch,
        2 * count * list_rows * width * (hidden_all + rows),
        2 * count * hidden_all * width,
    )


def wide_gather(block, width, pieces):
    count = lax.axis_size("wide")
    blocks = [block]
    for _ in range(1, count - 1):
        blocks.append(pass_on(blocks[-1], 1))
    last = split_block(blocks[-1], width, pieces)
    if count == 1:
        return [], last
    far = []
    for part in last:
        far.append(pass_on(part, 1))
    return blocks, far


def fold_body(own_ref, *refs, top):
    received, total_ref = refs[: -1 - top], refs[-1 - top]
    total = own_ref[...]
    for ref in received:
        total = total + ref[0].astype(jnp.float32)
    total_ref[...] = total.reshape(total_ref.shape)
    if top:
        refs[-1][...] = total[-refs[-1].shape[0] :].astype(jnp.bfloat16)


def add_body(total_ref, passed_ref, sum_ref, *, at):
    sum_ref[...] = (total_ref[at] + passed_ref[...].astype(jnp.float32)).astype(jnp.bfloat16)


def finish_body(*refs):
    out_ref, pieces = refs[-1], len(refs) // 2
    width = refs[0].shape[2]
    for h in range(pieces):
        mixed = refs[h][0] + refs[pieces + h][...].astype(jnp.float32)
        out_ref[:, h * width : (h + 1) * width] = mixed.astype(jnp.bfloat16)


def wide_return(sums, tok_rows, pieces, width):
    count = lax.axis_size("wide")
    part = array((tok_rows, width))
    passed = [None] * pieces
    for g, where in enumerate(distance_groups()):
        top = where.stop == count
        shape = (where.stop - where.start, tok_rows, width)
        totals = []
        for h in range(pieces):
            own, received = sums(g, h)
            result = call(
                functools.partial(fold_body, top=top),
                (array(shape, jnp.float32),) + (part,) * top,
                (own, *received),
                "v" * (1 + len(received)),
            )
            totals.append(result[0] if top else result)
            if top:
                passed[h] = result[1]
        for d in reversed(range(max(where.start, 1), where.stop)):
            for h in range(pieces):
                if d < count - 1:
                    passed[h] = call(
                        functools.partial(add_body, at=d - where.start),
                        part,
                        (totals[h], passed[h]),
                        "vv",
                    )
                passed[h] = pass_on(passed[h], -1)
    return call(
        finish_body, array((tok_rows, pieces * width)), (*totals, *passed), "v" * (2 * pieces)
    )


def gather_plan(tokens, route_logits, expert_ids, gate_weight, up_weight, down_weight):
    tok_rows, feature_part = tokens.shape
    top_count = expert_ids.shape[1]
    wide_count = lax.axis_size("wide")
    section_count = lax.axis_size("section")
    narrow_count = lax.axis_size("narrow")
    per_owner = gate_weight.shape[0]
    narrow_at = lax.axis_index("narrow").astype(jnp.int32).reshape(1)
    owner = lax.axis_index("wide") * section_count + lax.axis_index("section")
    base = (owner * per_owner).astype(jnp.int32).reshape(1)
    narrow_at, base, tokens = lax.optimization_barrier((narrow_at, base, tokens))
    gate_weight, up_weight = [
        pltpu.with_memory_space_constraint(w, pltpu.HBM) for w in (gate_weight, up_weight)
    ]
    pieces = 2
    width = feature_part // pieces
    list_rows = wide_count * section_count * CAP
    block = pack(tokens, route_logits, expert_ids, width)
    near, far = wide_gather(block, width, pieces)
    chunks = {}
    for j in range(narrow_count):
        side, last = near, far
        if j:
            side, last = [], []
            for b in near:
                side.append(shift(b, "narrow", j))
            for b in far:
                last.append(shift(b, "narrow", j))
        start = 0
        for q in range(pieces):
            stack = stack_blocks(side, last[q], start)
            start += last[q].shape[1]
            chunks[j, q] = [stack]
            for k in range(1, section_count):
                chunks[j, q].append(shift(stack, "section", k))
    order = [(j, q) for j in range(narrow_count) for q in range(pieces)]
    held = {}

    def fetch_of(key, first=0, count=per_owner):
        return gate_up_fetch(gate_weight, up_weight, width, *key, narrow_count, first, count)

    early = per_owner // 2
    late = per_owner - early
    whole, halves = [(0, per_owner)], [(0, early), (early, late)]
    for i, key in enumerate(order[:-1]):
        held[key] = []
        for first, count in halves if i else whole:
            fetch = fetch_of(key, first, count)
            held[key].append(call(None, (), (narrow_at,), "s", fetch=fetch))
    place, share, *picks = routing(narrow_at, base, chunks[0, 0], per_owner, tok_rows, top_count)
    sums = None
    for i, key in enumerate(order[:-1]):
        fetch = None if i else fetch_of(order[-1], 0, early)
        sums = gate_up(narrow_at, chunks[key], picks, held[key], sums, width, fetch=fetch)
        if fetch:
            sums, more = sums
            held[order[-1]] = [more]
    key = order[-1]
    hidden = [[[] for _ in range(narrow_count)] for _ in distance_groups()]
    weights, joined = held[key], ()
    for i, first in enumerate((0, early)):
        fetch = None if i else fetch_of(key, early, late)
        mine = gate_up(
            narrow_at, chunks[key], picks, weights, sums, width, first, True, joined, fetch
        )
        if fetch:
            *mine, rest = mine
            weights, joined = [rest], mine[1:]
        for g, h in enumerate(mine if i else mine[:1]):
            hidden[g][0].append(h)
            for k in range(1, narrow_count):
                hidden[g][k].append(shift(h, "narrow", k))
    combine = combine_tables(place, share, list_rows)

    half = own_half(narrow_at, hidden[0][0], down_weight)

    def sums(g, h):
        own, send = down(
            narrow_at,
            hidden[g],
            down_weight,
            combine[g],
            h * width,
            width,
            section_count,
            None if g else half,
        )
        received = []
        for k in range(1, section_count):
            received.append(shift(send[k - 1 : k], "section", section_count - k))
        return own, received

    return wide_return(sums, tok_rows, pieces, width)


def shards(tokens, route_logits, expert_ids, gate_weight, up_weight, down_weight):
    owners = lax.axis_size("wide") * lax.axis_size("section")
    per_owner = gate_weight.shape[0]
    whole_rows = per_owner * CAP >= tokens.shape[0]
    exact_ids = owners * per_owner <= 256
    args = (tokens, route_logits, expert_ids, gate_weight, up_weight, down_weight)
    chunks = 2 * lax.axis_size("narrow")
    even = tokens.shape[1] % (2 * TILE) == 0
    fits = even and chunks >= 4 and per_owner >= 2 and 16 * gate_weight.size // chunks <= RESIDENT
    if not (whole_rows and exact_ids and fits):
        return slot_plan(*args)
    return gather_plan(*args)


def solution(mesh):
    in_specs = (
        P(("groups", "wide", "section"), "narrow"),
        P(("groups", "wide", "section"), None),
        P(("groups", "wide", "section"), None),
        P(("wide", "section"), None, "narrow"),
        P(("wide", "section"), None, "narrow"),
        P(("wide", "section"), None, "narrow"),
    )
    out_specs = P(("groups", "wide", "section"), "narrow")
    return jax.shard_map(shards, mesh=mesh, in_specs=in_specs, out_specs=out_specs, check_vma=False)
```
